32 devices in a mesh: groups: 2 (over x), seq: 16 (over z, y, core).
Axes of the slice: x: 2, y: 2, z: 4, core: 2. Of those that a mesh axis runs over, the one named last changes fastest.
Arguments:
- features: bfloat16 [4, 16384, 384], P('groups', 'seq'), parts along dimension 0, may hold values from -6 to 6
- first_expand: bfloat16 [768, 1536], replicated, may hold values from -0.21875 to 0.21875
- first_contract: bfloat16 [1536, 768], replicated, may hold values from -0.15625 to 0.15625
- first_gain: float32 [1536], replicated, may hold values from 0.25 to 1.75
- first_shift: float32 [1536], replicated, may hold values from -3 to 3
- first_keep: float32 [768], replicated, may hold values from -1 to 2
- first_bias: float32 [768], replicated, may hold values from -2 to 2
- second_expand: bfloat16 [768, 1536], replicated, may hold values from -0.21875 to 0.21875
- second_contract: bfloat16 [1536, 768], replicated, may hold values from -0.15625 to 0.15625
- second_gain: float32 [1536], replicated, may hold values from 0.25 to 1.75
- second_shift: float32 [1536], replicated, may hold values from -3 to 3
- second_keep: float32 [768], replicated, may hold values from -1 to 2
- second_bias: float32 [768], replicated, may hold values from -2 to 2
Outputs:
- mixed: bfloat16 [4, 16384, 384], P('groups', 'seq'), parts along dimension 0
The draws below stay inside these ranges and needn't reach their ends.
There are 2 independent parts, one for each index of `groups`. The reference program is written for one: setup_inputs(seed, part) draws one part's arguments, and reference() takes and returns one part's arrays. A program takes and returns all parts, laid end to end along the dimension named above; an argument that names none is the same for every part. Nothing has to cross between parts.
All inputs are finite; a program needn't handle non-finite values.
Results may differ from the reference program's by a relative error of at most 0.0057.
Values may be sent and summed in bfloat16 or wider, within the bound.
No kernel may reach another device: no remote copies, remote signals or barrier semaphores. Data moves between devices by JAX's collectives and lax.ppermute only.
A program may use at most 64 MiB of HBM per device.

```python
import jax
import jax.numpy as jnp
from jax import lax

D = 384
H = 1536
ROWS_DEV = 1024
SHARDS = 16
ROWS = 16384


def block_levels(key, shape, pieces, least, largest):
    factor_of = 1.0
    for axis_at, blocks in pieces:
        steps = jax.random.uniform(jax.random.fold_in(jax.random.fold_in(key, 6), axis_at), (blocks,), jnp.float32, least / len(pieces), largest / len(pieces))
        factor_of = factor_of * jnp.repeat(jnp.exp(steps), shape[axis_at] // blocks).reshape((-1,) + (1,) * (len(shape) - 1 - axis_at))
    return factor_of


def normal_values(stream_key, dims, scale, bound, pieces=(), dtype=jnp.bfloat16):
    values = scale * jax.random.normal(stream_key, dims, jnp.float32)
    if pieces:
        values = values * block_levels(stream_key, dims, pieces, -0.22, 0.18)
    return jnp.clip(values, -bound, bound).astype(dtype)


def setup_inputs(seed: int = 0, part: int = 0) -> dict:
    key_of = jax.random.split(jax.random.key(seed), 14)
    part_splits = jax.random.split(jax.random.fold_in(key_of[13], part), 14)
    return {
        "features": normal_values(part_splits[0], (2, ROWS, D), 1.0, 6.0, ((1, 16),)),
        "first_expand": normal_values(key_of[1], (2 * D, H), (2 * D) ** -0.5, 0.21875),
        "first_contract": normal_values(key_of[2], (H, 2 * D), H ** -0.5, 0.15625),
        "first_gain": jnp.clip(1.0 + 0.15 * jax.random.normal(key_of[3], (H,), jnp.float32), 0.25, 1.75),
        "first_shift": normal_values(key_of[4], (H,), 0.5, 3.0, (), jnp.float32),
        "first_keep": jnp.clip(jax.random.uniform(key_of[5], (2 * D,), jnp.float32, -1.0, 2.0), -1.0, 2.0),
        "first_bias": normal_values(key_of[6], (2 * D,), 0.3, 2.0, (), jnp.float32),
        "second_expand": normal_values(key_of[7], (2 * D, H), (2 * D) ** -0.5, 0.21875),
        "second_contract": normal_values(key_of[8], (H, 2 * D), H ** -0.5, 0.15625),
        "second_gain": jnp.clip(1.0 + 0.15 * jax.random.normal(key_of[9], (H,), jnp.float32), 0.25, 1.75),
        "second_shift": normal_values(key_of[10], (H,), 0.5, 3.0, (), jnp.float32),
        "second_keep": jnp.clip(jax.random.uniform(key_of[11], (2 * D,), jnp.float32, -1.0, 2.0), -1.0, 2.0),
        "second_bias": normal_values(key_of[12], (2 * D,), 0.3, 2.0, (), jnp.float32),
    }


def switch_unit(pairs, expand, contract, gain, shift, keep, bias):
    width = pairs.shape[-1]
    flat = pairs.reshape(-1, width)
    hidden = jnp.dot(flat, expand, preferred_element_type=jnp.float32)
    center = hidden - lax.optimization_barrier(jnp.mean(hidden, axis=-1, keepdims=True))
    spread = lax.optimization_barrier(jnp.mean(center * center, axis=-1, keepdims=True))
    normed = center * lax.rsqrt(spread + 1e-05) * gain + shift
    active = jax.nn.gelu(normed).astype(jnp.bfloat16)
    result = jax.nn.sigmoid(keep) * flat.astype(jnp.float32) + jnp.dot(active, contract, preferred_element_type=jnp.float32) + bias
    return result.astype(jnp.bfloat16).reshape(pairs.shape)

def blocked(pairs, params):
    width = pairs.shape[-1]
    flat = pairs.reshape(-1, 4096, width)
    out = lax.map(lambda block: switch_unit(block, *params), flat)
    return out.reshape(pairs.shape)

def reference(features, first_expand, first_contract, first_gain, first_shift, first_keep, first_bias, second_expand, second_contract, second_gain, second_shift, second_keep, second_bias):
    width = features.shape[-1]
    clusters = ROWS // (16 * ROWS_DEV)
    grouped = features.reshape(2, clusters, 2, 8 * ROWS_DEV, width)
    pairs = jnp.concatenate([grouped[:, :, 0], grouped[:, :, 1]], axis=-1)
    out = blocked(pairs, (first_expand, first_contract, first_gain, first_shift, first_keep, first_bias))
    first = jnp.stack([out[..., :width], out[..., width:]], axis=2).reshape(2, ROWS, width)
    blocks = first.reshape(2, SHARDS, ROWS_DEV // SHARDS, SHARDS, width)
    shuffled = jnp.transpose(blocks, (0, 3, 2, 1, 4)).reshape(2, ROWS, width)
    pairs = shuffled.reshape(2, ROWS // 2, 2 * width)
    out = blocked(pairs, (second_expand, second_contract, second_gain, second_shift, second_keep, second_bias))
    return out.reshape(2, ROWS, width)
```

```python
import jax
import jax.numpy as jnp
from jax import lax
from jax.sharding import PartitionSpec as P

REACH = 8


def switch_unit(flat, expand, contract, gain, shift, keep, bias):
    hidden = jnp.dot(flat, expand, preferred_element_type=jnp.float32)
    center = hidden - jnp.mean(hidden, axis=-1, keepdims=True)
    spread = jnp.mean(center * center, axis=-1, keepdims=True)
    normed = center * lax.rsqrt(spread + 1e-05) * gain + shift
    active = jax.nn.gelu(normed).astype(jnp.bfloat16)
    result = (
        jax.nn.sigmoid(keep) * flat.astype(jnp.float32)
        + jnp.dot(active, contract, preferred_element_type=jnp.float32)
        + bias
    )
    return result.astype(jnp.bfloat16)


def per_device(features, *params):
    first_params, second_params = params[:6], params[6:]
    streams, rows_here, width = features.shape
    devices = lax.axis_size("seq")
    slots = rows_here // devices
    outgoing = features.reshape(streams, slots, devices, width).transpose(2, 0, 1, 3)
    outgoing = outgoing.reshape(devices, streams * slots, width)
    received = lax.all_to_all(outgoing, "seq", split_axis=0, concat_axis=0, tiled=True)
    clusters = devices // (2 * REACH)
    halves = received.reshape(clusters, 2, REACH, streams * slots, width)
    pairs = jnp.concatenate([halves[:, 0], halves[:, 1]], axis=-1).reshape(-1, 2 * width)
    mid = switch_unit(pairs, *first_params)
    mid = mid.reshape(clusters, REACH // 2, 2, streams * slots, 2, width)
    pairs = mid.transpose(0, 4, 1, 3, 2, 5).reshape(-1, 2 * width)
    result = switch_unit(pairs, *second_params)
    result = result.reshape(devices // 2, streams, slots, 2, width)
    return result.transpose(1, 2, 0, 3, 4).reshape(streams, rows_here, width)


def solution(mesh):
    return jax.shard_map(
        per_device,
        mesh=mesh,
        in_specs=(P("groups", "seq", None),) + (P(),) * 12,
        out_specs=P("groups", "seq", None),
        check_vma=False,
    )
```

```python
import functools

import jax
import jax.numpy as jnp
from jax import lax
from jax.experimental import pallas as pl
from jax.experimental.pallas import tpu as pltpu
from jax.sharding import PartitionSpec as P

REACH = 8
MIB = 1 << 20


def gelu(n):
    root = 0.7978845608028654
    half = 0.5 * n
    return half + half * jnp.tanh(n * (root + (root * 0.044715) * (n * n)))


def switch_rows(s, expand, contract, wide, narrow):
    hidden = jnp.dot(s, expand, preferred_element_type=jnp.float32)
    center = hidden - jnp.mean(hidden, axis=-1, keepdims=True)
    spread = jnp.mean(center * center, axis=-1, keepdims=True)
    normed = center * lax.rsqrt(spread + 1e-05) * wide[0:1] + wide[1:2]
    active = gelu(normed).astype(jnp.bfloat16)
    result = (
        narrow[0:1] * s.astype(jnp.float32)
        + jnp.dot(active, contract, preferred_element_type=jnp.float32)
        + narrow[1:2]
    )
    return result.astype(jnp.bfloat16)


def iota2(shape, dim):
    return lax.broadcasted_iota(jnp.int32, shape, dim)


def one_hot(hit):
    return jnp.where(hit, 1.0, 0.0).astype(jnp.bfloat16)


def sort_kernel(shards, x_ref, *outs):
    me = lax.axis_index("seq")
    tile = shards * shards
    row, col = iota2((tile, tile), 0), iota2((tile, tile), 1)
    pick = one_hot((col // shards == row % shards) & (col % shards == ((row // shards) ^ me)))
    streams, rows, _ = x_ref.shape
    for s in range(streams):
        for t in range(rows // tile):
            y = jnp.dot(pick, x_ref[s, t * tile : (t + 1) * tile], preferred_element_type=jnp.float32)
            y = y.astype(jnp.bfloat16)
            at = s * (rows // shards) + t * shards
            for mask in range(shards):
                outs[mask][at : at + shards] = y[mask * shards : (mask + 1) * shards]


def sort_rows(features, shards):
    streams, rows, width = features.shape
    block = jax.ShapeDtypeStruct((streams * rows // shards, width), features.dtype)
    return pl.pallas_call(
        functools.partial(sort_kernel, shards),
        out_shape=[block] * shards,
        in_specs=[pl.BlockSpec(memory_space=pltpu.VMEM)],
        out_specs=[pl.BlockSpec(memory_space=pltpu.VMEM)] * shards,
        compiler_params=pltpu.CompilerParams(vmem_limit_bytes=16 * MIB),
        cost_estimate=pl.CostEstimate(flops=10**9, bytes_accessed=2 * features.size * 2, transcendentals=0),
        name="sort_rows",
    )(features)


def group_blocks(refs, roles, first, second):
    me = lax.axis_index("seq")
    core, upper = me & 1, (me // REACH) & 1
    for i, ref in enumerate(refs):
        roles[(upper ^ (i // 2)) * 2 + (core ^ (i % 2))] = ref[...]
    first = [ref[...] for ref in first]
    second = [ref[...] for ref in second]
    width = roles.shape[-1]
    mids = [
        switch_rows(jnp.concatenate([roles[c], roles[2 + c]], axis=-1), *first) for c in range(2)
    ]
    ends = []
    for half in range(2):
        part = slice(half * width, (half + 1) * width)
        o = switch_rows(jnp.concatenate([mids[0][:, part], mids[1][:, part]], axis=-1), *second)
        ends += [o[:, :width], o[:, width:]]
    return ends


def group_kernel(*refs):
    blocks, first, second, out, roles = refs[:4], refs[4:8], refs[8:12], refs[12], refs[13]
    for i, end in enumerate(group_blocks(blocks, roles, first, second)):
        out[i] = end


def last_kernel(shards, groups, *refs):
    blocks, first, second = refs[:4], refs[4:8], refs[8:12]
    done, out, roles = refs[12 : 12 + groups - 1], refs[12 + groups - 1], refs[12 + groups]
    ends = group_blocks(blocks, roles, first, second)
    me = lax.axis_index("seq")
    near = (me & (REACH - 1)) >> 1
    tile = shards * shards
    row, col = iota2((tile, tile), 0), iota2((tile, tile), 1)
    group, half, core = col // (4 * shards), (col // (2 * shards)) % 2, (col // shards) % 2
    source = half * REACH + ((group ^ near) * 2 + core)
    place = one_hot((row // shards == col % shards) & (row % shards == source))
    streams, rows, _ = out.shape
    for s in range(streams):
        for t in range(rows // tile):
            at = s * (rows // shards) + t * shards
            parts = [d[i, at : at + shards] for d in done for i in range(4)]
            parts += [end[at : at + shards] for end in ends]
            y = jnp.dot(place, jnp.concatenate(parts, axis=0), preferred_element_type=jnp.float32)
            out[s, t * tile : (t + 1) * tile] = y.astype(jnp.bfloat16)


def run_group(kernel, blocks, params, extra, out_shape, name):
    rows, width = blocks[0].shape
    args = (*blocks, *params, *extra)
    hidden = params[0].shape[1]
    return pl.pallas_call(
        kernel,
        out_shape=out_shape,
        in_specs=[pl.BlockSpec(memory_space=pltpu.VMEM)] * len(args),
        out_specs=pl.BlockSpec(memory_space=pltpu.VMEM),
        scratch_shapes=[pltpu.VMEM((4, rows, width), jnp.bfloat16)],
        compiler_params=pltpu.CompilerParams(vmem_limit_bytes=32 * MIB),
        cost_estimate=pl.CostEstimate(
            flops=2 * 2 * rows * 4 * 2 * width * hidden,
            bytes_accessed=sum(a.size * a.dtype.itemsize for a in args),
            transcendentals=4 * rows * hidden,
        ),
        name=name,
    )(*args)


def packed(params):
    expand, contract, gain, shift, keep, bias = params
    return expand, contract, jnp.stack([gain, shift]), jnp.stack([jax.nn.sigmoid(keep), bias])


def exchanged(features, params, shards):
    sent = sort_rows(features, shards)
    groups = REACH // 2
    waves = [[REACH], [REACH + 1, 1]]
    for g in range(1, groups):
        waves += [[REACH + 2 * g, 2 * g], [REACH + 2 * g + 1, 2 * g + 1]]
    window = 4
    got, ends = {0: sent[0]}, []
    for i, wave in enumerate(waves):
        ops = [sent[mask] for mask in wave]
        if i >= window:
            before = waves[i - window]
            hold = [got[mask] for mask in before]
            extra = []
            held = lax.optimization_barrier((*ops, *hold, *extra))
            ops = list(held[: len(ops)])
            for mask, value in zip(before, held[len(ops) :]):
                got[mask] = value
        for mask, op in zip(wave, ops):
            pairs = [(d, d ^ mask) for d in range(shards)]
            got[mask] = lax.ppermute(op, "seq", pairs)
    for g in range(groups):
        blocks = [got[2 * g], got[2 * g + 1], got[REACH + 2 * g], got[REACH + 2 * g + 1]]
        if g < groups - 1:
            shape = jax.ShapeDtypeStruct((4, *blocks[0].shape), features.dtype)
            ends.append(run_group(group_kernel, blocks, params, (), shape, "switch_group"))
        else:
            kernel = functools.partial(last_kernel, shards, groups)
            shape = jax.ShapeDtypeStruct(features.shape, features.dtype)
            return run_group(kernel, blocks, params, tuple(ends), shape, "switch_last")


def switch_unit(flat, expand, contract, wide, narrow):
    return switch_rows(flat, expand, contract, wide, narrow)


def gathered(features, first, second):
    streams, rows_here, width = features.shape
    devices = lax.axis_size("seq")
    slots = rows_here // devices
    outgoing = features.reshape(streams, slots, devices, width).transpose(2, 0, 1, 3)
    outgoing = outgoing.reshape(devices, streams * slots, width)
    received = lax.all_to_all(outgoing, "seq", split_axis=0, concat_axis=0, tiled=True)
    clusters = devices // (2 * REACH)
    halves = received.reshape(clusters, 2, REACH, streams * slots, width)
    pairs = jnp.concatenate([halves[:, 0], halves[:, 1]], axis=-1).reshape(-1, 2 * width)
    mid = switch_unit(pairs, *first)
    mid = mid.reshape(clusters, REACH // 2, 2, streams * slots, 2, width)
    pairs = mid.transpose(0, 4, 1, 3, 2, 5).reshape(-1, 2 * width)
    result = switch_unit(pairs, *second)
    result = result.reshape(devices // 2, streams, slots, 2, width)
    return result.transpose(1, 2, 0, 3, 4).reshape(streams, rows_here, width)


def per_device(features, *params):
    first, second = packed(params[:6]), packed(params[6:])
    shards = lax.axis_size("seq")
    if shards == 2 * REACH and features.shape[1] % (shards * shards) == 0:
        return exchanged(features, (*first, *second), shards)
    return gathered(features, first, second)


def solution(mesh):
    return jax.shard_map(
        per_device,
        mesh=mesh,
        in_specs=(P("groups", "seq", None),) + (P(),) * 12,
        out_specs=P("groups", "seq", None),
        check_vma=False,
    )
```

```python
import functools

import jax
import jax.numpy as jnp
from jax import lax
from jax.experimental import pallas as pl
from jax.experimental.pallas import tpu as pltpu
from jax.sharding import PartitionSpec as P

REACH = 8
WEIGH = (0, 0, 1)
MIB = 1 << 20


def gelu(n):
    root = 0.7978845608028654
    half = 0.5 * n
    return half + half * jnp.tanh(n * (root + (root * 0.044715) * (n * n)))


def switch_rows(s, expand, contract, gain, shift, keep, bias):
    hidden = jnp.dot(s, expand, preferred_element_type=jnp.float32)
    center = hidden - jnp.mean(hidden, axis=-1, keepdims=True)
    spread = jnp.mean(center * center, axis=-1, keepdims=True)
    normed = center * lax.rsqrt(spread + 1e-05) * gain[None] + shift[None]
    active = gelu(normed).astype(jnp.bfloat16)
    result = (
        jax.nn.sigmoid(keep[None]) * s.astype(jnp.float32)
        + jnp.dot(active, contract, preferred_element_type=jnp.float32)
        + bias[None]
    )
    return result.astype(jnp.bfloat16)


def iota2(shape, dim):
    return lax.broadcasted_iota(jnp.int32, shape, dim)


def one_hot(hit):
    return jnp.where(hit, 1.0, 0.0).astype(jnp.bfloat16)


def sort_kernel(shards, x_ref, straight, mate, ahead, first, second):
    me = lax.axis_index("seq")
    tile = shards * shards
    streams, rows, _ = x_ref.shape
    row, col = iota2((tile, tile), 0), iota2((tile, tile), 1)
    pick = one_hot((col // shards == row % shards) & (col % shards == ((row // shards) ^ me)))
    for s in range(streams):
        for t in range(rows // tile):
            y = jnp.dot(pick, x_ref[s, t * tile : (t + 1) * tile], preferred_element_type=jnp.float32)
            y = y.astype(jnp.bfloat16)
            at = s * (rows // shards) + t * shards
            for mask in range(shards):
                part = y[mask * shards : (mask + 1) * shards]
                if mask == 0:
                    straight[at : at + shards] = part
                elif mask == REACH:
                    first[at : at + shards] = part
                elif mask == REACH + 1:
                    second[at : at + shards] = part
                elif mask % 2:
                    mate[mask_slot(mask), at : at + shards] = part
                else:
                    ahead[mask_slot(mask) - 1, at : at + shards] = part


def mask_slot(mask):
    chip = mask // 2
    return chip if chip < REACH // 2 else chip - 1


def sort_rows(features, shards):
    streams, rows, width = features.shape
    count = streams * rows // shards
    block = jax.ShapeDtypeStruct((count, width), features.dtype)
    mate = jax.ShapeDtypeStruct((REACH - 1, count, width), features.dtype)
    ahead = jax.ShapeDtypeStruct((REACH - 2, count, width), features.dtype)
    return pl.pallas_call(
        functools.partial(sort_kernel, shards),
        out_shape=[block, mate, ahead, block, block],
        in_specs=[pl.BlockSpec(memory_space=pltpu.VMEM)],
        out_specs=[pl.BlockSpec(memory_space=pltpu.VMEM)] * 5,
        compiler_params=pltpu.CompilerParams(vmem_limit_bytes=16 * MIB),
        cost_estimate=pl.CostEstimate(flops=3 * 10**10, bytes_accessed=2 * features.size * 2, transcendentals=0),
        name="sort_rows",
    )(features)


def join_kernel(straight, mate, ahead, *outs):
    count = straight.shape[0]
    for i, out in enumerate(outs):
        out[:count] = straight[...] if i == 0 else ahead[i - 1]
        out[count:] = mate[i]


def join_rows(straight, mate, ahead):
    count, width = straight.shape
    pair = jax.ShapeDtypeStruct((2 * count, width), straight.dtype)
    return pl.pallas_call(
        join_kernel,
        out_shape=[pair] * (REACH - 1),
        in_specs=[pl.BlockSpec(memory_space=pltpu.VMEM)] * 3,
        out_specs=[pl.BlockSpec(memory_space=pltpu.VMEM)] * (REACH - 1),
        compiler_params=pltpu.CompilerParams(vmem_limit_bytes=16 * MIB),
        cost_estimate=pl.CostEstimate(flops=0, bytes_accessed=4 * mate.size * 2, transcendentals=0),
        name="join_rows",
    )(straight, mate, ahead)


def group_blocks(refs, roles, first, second):
    me = lax.axis_index("seq")
    core, upper = me & 1, (me // REACH) & 1
    count = roles.shape[1]
    parts = [(ref, at) for ref in refs for at in range(0, ref.shape[0], count)]
    for i, (ref, at) in enumerate(parts):
        roles[(upper ^ (i // 2)) * 2 + (core ^ (i % 2))] = ref[at : at + count]
    first = [ref[...] for ref in first]
    second = [ref[...] for ref in second]
    width = roles.shape[-1]
    mids = [
        switch_rows(jnp.concatenate([roles[c], roles[2 + c]], axis=-1), *first) for c in range(2)
    ]
    ends = []
    for half in range(2):
        part = slice(half * width, (half + 1) * width)
        o = switch_rows(jnp.concatenate([mids[0][:, part], mids[1][:, part]], axis=-1), *second)
        ends += [o[:, :width], o[:, width:]]
    return ends


def group_kernel(blocks, *refs):
    first, second, out, roles = refs[blocks : blocks + 6], refs[blocks + 6 : blocks + 12], refs[-2], refs[-1]
    for i, end in enumerate(group_blocks(refs[:blocks], roles, first, second)):
        out[i] = end


def last_kernel(blocks, shards, *refs):
    first, second = refs[blocks : blocks + 6], refs[blocks + 6 : blocks + 12]
    done, out, roles = refs[blocks + 12 : -2], refs[-2], refs[-1]
    ends = group_blocks(refs[:blocks], roles, first, second)
    me = lax.axis_index("seq")
    near = (me & (REACH - 1)) >> 1
    tile = shards * shards
    row, col = iota2((tile, tile), 0), iota2((tile, tile), 1)
    group, half, core = col // (4 * shards), (col // (2 * shards)) % 2, (col // shards) % 2
    source = half * REACH + ((group ^ near) * 2 + core)
    place = one_hot((row // shards == col % shards) & (row % shards == source))
    streams, rows, _ = out.shape
    for s in range(streams):
        for t in range(rows // tile):
            at = s * (rows // shards) + t * shards
            parts = [d[i, at : at + shards] for d in done for i in range(4)]
            parts += [end[at : at + shards] for end in ends]
            y = jnp.dot(place, jnp.concatenate(parts, axis=0), preferred_element_type=jnp.float32)
            out[s, t * tile : (t + 1) * tile] = y.astype(jnp.bfloat16)


def run_group(kernel, blocks, count, params, extra, out_shape, name, weigh=1):
    width = blocks[0].shape[-1]
    args = (*blocks, *params, *extra)
    hidden = params[0].shape[1]
    return pl.pallas_call(
        functools.partial(kernel, len(blocks)),
        out_shape=out_shape,
        in_specs=[pl.BlockSpec(memory_space=pltpu.VMEM)] * len(args),
        out_specs=pl.BlockSpec(memory_space=pltpu.VMEM),
        scratch_shapes=[pltpu.VMEM((4, count, width), jnp.bfloat16)],
        compiler_params=pltpu.CompilerParams(vmem_limit_bytes=32 * MIB),
        cost_estimate=pl.CostEstimate(
            flops=weigh * 2 * 2 * count * 4 * 2 * width * hidden,
            bytes_accessed=weigh * sum(a.size * a.dtype.itemsize for a in args),
            transcendentals=weigh * 4 * count * hidden,
        ),
        name=name,
    )(*args)


def after(values, *before):
    held = lax.optimization_barrier((*values, *before))
    return held[: len(values)]


def exchanged(features, params, shards):
    def send(value, mask):
        return lax.ppermute(value, "seq", [(d, d ^ mask) for d in range(shards)])

    straight, mate, ahead, far0, far1 = sort_rows(features, shards)
    count = straight.shape[0]
    groups = REACH // 2
    far0, far1 = send(far0, REACH), send(far1, REACH + 1)
    joined = join_rows(straight, send(mate, 1), ahead)
    near = list(joined[:groups])
    far = [None, *joined[groups:]]
    block = jax.ShapeDtypeStruct((4, count, features.shape[-1]), features.dtype)

    def group(index):
        near_rows, far_rows = arrived[index]
        return run_group(
            group_kernel, (near_rows, *far_rows), count, params, (), block, "switch_group", WEIGH[index]
        )

    ends = []
    arrived = [(near[0], (far0, far1))]
    arrived.append((send(near[1], 2), (send(far[1], REACH + 2),)))
    for g in range(2, groups):
        past_near, past_far = arrived[g - 2]
        near_next, far_next, past_near, *past_far = after((near[g], far[g], past_near, *past_far), *ends[:g - 1])
        arrived[g - 2] = (past_near, tuple(past_far))
        arrived.append((send(near_next, 2 * g), (send(far_next, REACH + 2 * g),)))
        ends.append(group(g - 2))
    ends.append(group(groups - 2))
    near_rows, far_rows = arrived[groups - 1]
    whole = jax.ShapeDtypeStruct(features.shape, features.dtype)

    def kernel(blocks, *refs):
        last_kernel(blocks, shards, *refs)

    return run_group(kernel, (near_rows, *far_rows), count, params, tuple(ends), whole, "switch_last")


def gathered(features, first, second):
    streams, rows_here, width = features.shape
    devices = lax.axis_size("seq")
    slots = rows_here // devices
    outgoing = features.reshape(streams, slots, devices, width).transpose(2, 0, 1, 3)
    outgoing = outgoing.reshape(devices, streams * slots, width)
    received = lax.all_to_all(outgoing, "seq", split_axis=0, concat_axis=0, tiled=True)
    clusters = devices // (2 * REACH)
    halves = received.reshape(clusters, 2, REACH, streams * slots, width)
    pairs = jnp.concatenate([halves[:, 0], halves[:, 1]], axis=-1).reshape(-1, 2 * width)
    mid = switch_rows(pairs, *first)
    mid = mid.reshape(clusters, REACH // 2, 2, streams * slots, 2, width)
    pairs = mid.transpose(0, 4, 1, 3, 2, 5).reshape(-1, 2 * width)
    result = switch_rows(pairs, *second)
    result = result.reshape(devices // 2, streams, slots, 2, width)
    return result.transpose(1, 2, 0, 3, 4).reshape(streams, rows_here, width)


def per_device(features, *params):
    first, second = params[:6], params[6:]
    shards = lax.axis_size("seq")
    if shards == 2 * REACH and features.shape[1] % (shards * shards) == 0:
        return exchanged(features, params, shards)
    return gathered(features, first, second)


def solution(mesh):
    return jax.shard_map(
        per_device,
        mesh=mesh,
        in_specs=(P("groups", "seq", None),) + (P(),) * 12,
        out_specs=P("groups", "seq", None),
        check_vma=False,
    )
```

```python
import functools

import jax
import jax.numpy as jnp
from jax import lax
from jax.experimental import pallas as pl
from jax.experimental.pallas import tpu as pltpu
from jax.sharding import PartitionSpec as P

REACH = 8
WEIGH = (0, 0, 1)
MIB = 1 << 20


def gelu(n):
    root = 0.7978845608028654
    half = 0.5 * n
    return half + half * jnp.tanh(n * (root + (root * 0.044715) * (n * n)))


def dot(a, b):
    return jnp.dot(a, b, preferred_element_type=jnp.float32)


def activated(hidden, gain, shift):
    center = hidden - jnp.mean(hidden, axis=-1, keepdims=True)
    spread = jnp.mean(center * center, axis=-1, keepdims=True)
    normed = center * lax.rsqrt(spread + 1e-05) * gain[None] + shift[None]
    return gelu(normed).astype(jnp.bfloat16)


def switch_tiles(tiles, expand, contract, gain, shift, keep, bias):
    keep = jax.nn.sigmoid(keep[None])
    hidden, results = [dot(tiles[0], expand)], []
    for i, s in enumerate(tiles):
        if i + 1 < len(tiles):
            hidden.append(dot(tiles[i + 1], expand))
        active = activated(hidden[i], gain, shift)
        result = keep * s.astype(jnp.float32) + dot(active, contract) + bias[None]
        results.append(result.astype(jnp.bfloat16))
    return results


def iota2(shape, dim):
    return lax.broadcasted_iota(jnp.int32, shape, dim)


def one_hot(hit):
    return jnp.where(hit, 1.0, 0.0).astype(jnp.bfloat16)


def sort_kernel(shards, x_ref, straight, mate, ahead, first, second):
    me = lax.axis_index("seq")
    tile = shards * shards
    streams, rows, _ = x_ref.shape
    row, col = iota2((tile, tile), 0), iota2((tile, tile), 1)
    pick = one_hot((col // shards == row % shards) & (col % shards == ((row // shards) ^ me)))
    for s in range(streams):
        for t in range(rows // tile):
            y = jnp.dot(pick, x_ref[s, t * tile : (t + 1) * tile], preferred_element_type=jnp.float32)
            y = y.astype(jnp.bfloat16)
            at = s * (rows // shards) + t * shards
            for mask in range(shards):
                part = y[mask * shards : (mask + 1) * shards]
                if mask == 0:
                    straight[at : at + shards] = part
                elif mask == REACH:
                    first[at : at + shards] = part
                elif mask == REACH + 1:
                    second[at : at + shards] = part
                elif mask % 2:
                    mate[mask_slot(mask), at : at + shards] = part
                else:
                    ahead[mask_slot(mask) - 1, at : at + shards] = part


def mask_slot(mask):
    chip = mask // 2
    return chip if chip < REACH // 2 else chip - 1


def sort_rows(features, shards):
    streams, rows, width = features.shape
    count = streams * rows // shards
    block = jax.ShapeDtypeStruct((count, width), features.dtype)
    mate = jax.ShapeDtypeStruct((REACH - 1, count, width), features.dtype)
    ahead = jax.ShapeDtypeStruct((REACH - 2, count, width), features.dtype)
    return pl.pallas_call(
        functools.partial(sort_kernel, shards),
        out_shape=[block, mate, ahead, block, block],
        in_specs=[pl.BlockSpec(memory_space=pltpu.VMEM)],
        out_specs=[pl.BlockSpec(memory_space=pltpu.VMEM)] * 5,
        compiler_params=pltpu.CompilerParams(vmem_limit_bytes=16 * MIB),
        cost_estimate=pl.CostEstimate(flops=3 * 10**10, bytes_accessed=2 * features.size * 2, transcendentals=0),
        name="sort_rows",
    )(features)


def join_kernel(straight, mate, ahead, *outs):
    count = straight.shape[0]
    for i, out in enumerate(outs):
        out[:count] = straight[...] if i == 0 else ahead[i - 1]
        out[count:] = mate[i]


def join_rows(straight, mate, ahead):
    count, width = straight.shape
    pair = jax.ShapeDtypeStruct((2 * count, width), straight.dtype)
    return pl.pallas_call(
        join_kernel,
        out_shape=[pair] * (REACH - 1),
        in_specs=[pl.BlockSpec(memory_space=pltpu.VMEM)] * 3,
        out_specs=[pl.BlockSpec(memory_space=pltpu.VMEM)] * (REACH - 1),
        compiler_params=pltpu.CompilerParams(vmem_limit_bytes=16 * MIB),
        cost_estimate=pl.CostEstimate(flops=0, bytes_accessed=4 * mate.size * 2, transcendentals=0),
        name="join_rows",
    )(straight, mate, ahead)


def group_blocks(refs, roles, first, second):
    me = lax.axis_index("seq")
    core, upper = me & 1, (me // REACH) & 1
    count = roles.shape[1]
    parts = [(ref, at) for ref in refs for at in range(0, ref.shape[0], count)]
    for i, (ref, at) in enumerate(parts):
        roles[(upper ^ (i // 2)) * 2 + (core ^ (i % 2))] = ref[at : at + count]
    first = [ref[...] for ref in first]
    second = [ref[...] for ref in second]
    width = roles.shape[-1]
    mids = switch_tiles([jnp.concatenate([roles[c], roles[2 + c]], axis=-1) for c in range(2)], *first)
    halves = [slice(0, width), slice(width, 2 * width)]
    pairs = [jnp.concatenate([mids[0][:, part], mids[1][:, part]], axis=-1) for part in halves]
    return [o[:, part] for o in switch_tiles(pairs, *second) for part in halves]


def group_kernel(blocks, *refs):
    first, second, out, roles = refs[blocks : blocks + 6], refs[blocks + 6 : blocks + 12], refs[-2], refs[-1]
    for i, end in enumerate(group_blocks(refs[:blocks], roles, first, second)):
        out[i] = end


def last_kernel(blocks, shards, *refs):
    first, second = refs[blocks : blocks + 6], refs[blocks + 6 : blocks + 12]
    done, out, roles = refs[blocks + 12 : -2], refs[-2], refs[-1]
    ends = group_blocks(refs[:blocks], roles, first, second)
    me = lax.axis_index("seq")
    near = (me & (REACH - 1)) >> 1
    tile = shards * shards
    row, col = iota2((tile, tile), 0), iota2((tile, tile), 1)
    group, half, core = col // (4 * shards), (col // (2 * shards)) % 2, (col // shards) % 2
    source = half * REACH + ((group ^ near) * 2 + core)
    place = one_hot((row // shards == col % shards) & (row % shards == source))
    streams, rows, _ = out.shape
    for s in range(streams):
        for t in range(rows // tile):
            at = s * (rows // shards) + t * shards
            parts = [d[i, at : at + shards] for d in done for i in range(4)]
            parts += [end[at : at + shards] for end in ends]
            y = jnp.dot(place, jnp.concatenate(parts, axis=0), preferred_element_type=jnp.float32)
            out[s, t * tile : (t + 1) * tile] = y.astype(jnp.bfloat16)


def run_group(kernel, blocks, count, params, extra, out_shape, name, weigh=1):
    width = blocks[0].shape[-1]
    args = (*blocks, *params, *extra)
    hidden = params[0].shape[1]
    return pl.pallas_call(
        functools.partial(kernel, len(blocks)),
        out_shape=out_shape,
        in_specs=[pl.BlockSpec(memory_space=pltpu.VMEM)] * len(args),
        out_specs=pl.BlockSpec(memory_space=pltpu.VMEM),
        scratch_shapes=[pltpu.VMEM((4, count, width), jnp.bfloat16)],
        compiler_params=pltpu.CompilerParams(vmem_limit_bytes=32 * MIB),
        cost_estimate=pl.CostEstimate(
            flops=weigh * 2 * 2 * count * 4 * 2 * width * hidden,
            bytes_accessed=weigh * sum(a.size * a.dtype.itemsize for a in args),
            transcendentals=weigh * 4 * count * hidden,
        ),
        name=name,
    )(*args)


def after(values, *before):
    held = lax.optimization_barrier((*values, *before))
    return held[: len(values)]


def exchanged(features, params, shards):
    def send(value, mask):
        return lax.ppermute(value, "seq", [(d, d ^ mask) for d in range(shards)])

    straight, mate, ahead, far0, far1 = sort_rows(features, shards)
    count = straight.shape[0]
    groups = REACH // 2
    far0, far1 = send(far0, REACH), send(far1, REACH + 1)
    joined = join_rows(straight, send(mate, 1), ahead)
    near = list(joined[:groups])
    far = [None, *joined[groups:]]
    block = jax.ShapeDtypeStruct((4, count, features.shape[-1]), features.dtype)

    def group(index):
        near_rows, far_rows = arrived[index]
        return run_group(
            group_kernel, (near_rows, *far_rows), count, params, (), block, "switch_group", WEIGH[index]
        )

    ends = []
    arrived = [(near[0], (far0, far1))]
    arrived.append((send(near[1], 2), (send(far[1], REACH + 2),)))
    for g in range(2, groups):
        past_near, past_far = arrived[g - 2]
        near_next, far_next, past_near, *past_far = after((near[g], far[g], past_near, *past_far), *ends[:g - 1])
        arrived[g - 2] = (past_near, tuple(past_far))
        arrived.append((send(near_next, 2 * g), (send(far_next, REACH + 2 * g),)))
        ends.append(group(g - 2))
    ends.append(group(groups - 2))
    near_rows, far_rows = arrived[groups - 1]
    whole = jax.ShapeDtypeStruct(features.shape, features.dtype)

    def kernel(blocks, *refs):
        last_kernel(blocks, shards, *refs)

    return run_group(kernel, (near_rows, *far_rows), count, params, tuple(ends), whole, "switch_last")


def gathered(features, first, second):
    streams, rows_here, width = features.shape
    devices = lax.axis_size("seq")
    slots = rows_here // devices
    outgoing = features.reshape(streams, slots, devices, width).transpose(2, 0, 1, 3)
    outgoing = outgoing.reshape(devices, streams * slots, width)
    received = lax.all_to_all(outgoing, "seq", split_axis=0, concat_axis=0, tiled=True)
    clusters = devices // (2 * REACH)
    halves = received.reshape(clusters, 2, REACH, streams * slots, width)
    pairs = jnp.concatenate([halves[:, 0], halves[:, 1]], axis=-1).reshape(-1, 2 * width)
    (mid,) = switch_tiles([pairs], *first)
    mid = mid.reshape(clusters, REACH // 2, 2, streams * slots, 2, width)
    pairs = mid.transpose(0, 4, 1, 3, 2, 5).reshape(-1, 2 * width)
    (result,) = switch_tiles([pairs], *second)
    result = result.reshape(devices // 2, streams, slots, 2, width)
    return result.transpose(1, 2, 0, 3, 4).reshape(streams, rows_here, width)


def per_device(features, *params):
    first, second = params[:6], params[6:]
    shards = lax.axis_size("seq")
    if shards == 2 * REACH and features.shape[1] % (shards * shards) == 0:
        return exchanged(features, params, shards)
    return gathered(features, first, second)


def solution(mesh):
    return jax.shard_map(
        per_device,
        mesh=mesh,
        in_specs=(P("groups", "seq", None),) + (P(),) * 12,
        out_specs=P("groups", "seq", None),
        check_vma=False,
    )
```

```python
import functools

import jax
import jax.numpy as jnp
from jax import lax
from jax.experimental import pallas as pl
from jax.experimental.pallas import tpu as pltpu
from jax.sharding import PartitionSpec as P

REACH = 8
FIRSTS = (REACH, REACH + 1)
ORDER = ((10, ()), (2, ()), (12, (8,)), (4, (8, 9)), (14, (8, 9)), (6, (2, 10)))
WEIGH = (0, 0, 1)
MIB = 1 << 20


def gelu(n):
    root = 0.7978845608028654
    half = 0.5 * n
    return half + half * jnp.tanh(n * (root + (root * 0.044715) * (n * n)))


def dot(a, b):
    return jnp.dot(a, b, preferred_element_type=jnp.float32)


def activated(hidden, gain, shift):
    center = hidden - jnp.mean(hidden, axis=-1, keepdims=True)
    spread = jnp.mean(center * center, axis=-1, keepdims=True)
    normed = center * lax.rsqrt(spread + 1e-05) * gain[None] + shift[None]
    return gelu(normed).astype(jnp.bfloat16)


def switch_tiles(tiles, expand, contract, gain, shift, keep, bias):
    keep = jax.nn.sigmoid(keep[None])
    hidden, results = [dot(tiles[0], expand)], []
    for i, s in enumerate(tiles):
        if i + 1 < len(tiles):
            hidden.append(dot(tiles[i + 1], expand))
        active = activated(hidden[i], gain, shift)
        result = keep * s.astype(jnp.float32) + dot(active, contract) + bias[None]
        results.append(result.astype(jnp.bfloat16))
    return results


def iota2(shape, dim):
    return lax.broadcasted_iota(jnp.int32, shape, dim)


def one_hot(hit):
    return jnp.where(hit, 1.0, 0.0).astype(jnp.bfloat16)


def sort_kernel(shards, x_ref, straight, mate, ahead, first, second):
    me = lax.axis_index("seq")
    tile = shards * shards
    streams, rows, _ = x_ref.shape
    row, col = iota2((tile, tile), 0), iota2((tile, tile), 1)
    pick = one_hot((col // shards == row % shards) & (col % shards == ((row // shards) ^ me)))
    for s in range(streams):
        for t in range(rows // tile):
            y = jnp.dot(pick, x_ref[s, t * tile : (t + 1) * tile], preferred_element_type=jnp.float32)
            y = y.astype(jnp.bfloat16)
            at = s * (rows // shards) + t * shards
            for mask in range(shards):
                part = y[mask * shards : (mask + 1) * shards]
                if mask == 0:
                    straight[at : at + shards] = part
                elif mask == REACH:
                    first[at : at + shards] = part
                elif mask == REACH + 1:
                    second[at : at + shards] = part
                elif mask % 2:
                    mate[mask_slot(mask), at : at + shards] = part
                else:
                    ahead[mask_slot(mask) - 1, at : at + shards] = part


def mask_slot(mask):
    chip = mask // 2
    return chip if chip < REACH // 2 else chip - 1


def sort_rows(features, shards):
    streams, rows, width = features.shape
    count = streams * rows // shards
    block = jax.ShapeDtypeStruct((count, width), features.dtype)
    mate = jax.ShapeDtypeStruct((REACH - 1, count, width), features.dtype)
    ahead = jax.ShapeDtypeStruct((REACH - 2, count, width), features.dtype)
    return pl.pallas_call(
        functools.partial(sort_kernel, shards),
        out_shape=[block, mate, ahead, block, block],
        in_specs=[pl.BlockSpec(memory_space=pltpu.VMEM)],
        out_specs=[pl.BlockSpec(memory_space=pltpu.VMEM)] * 5,
        compiler_params=pltpu.CompilerParams(vmem_limit_bytes=16 * MIB),
        cost_estimate=pl.CostEstimate(flops=3 * 10**10, bytes_accessed=2 * features.size * 2, transcendentals=0),
        name="sort_rows",
    )(features)


def join_kernel(straight, mate, ahead, *outs):
    count = straight.shape[0]
    for i, out in enumerate(outs):
        out[:count] = straight[...] if i == 0 else ahead[i - 1]
        out[count:] = mate[i]


def join_rows(straight, mate, ahead):
    count, width = straight.shape
    pair = jax.ShapeDtypeStruct((2 * count, width), straight.dtype)
    return pl.pallas_call(
        join_kernel,
        out_shape=[pair] * (REACH - 1),
        in_specs=[pl.BlockSpec(memory_space=pltpu.VMEM)] * 3,
        out_specs=[pl.BlockSpec(memory_space=pltpu.VMEM)] * (REACH - 1),
        compiler_params=pltpu.CompilerParams(vmem_limit_bytes=16 * MIB),
        cost_estimate=pl.CostEstimate(flops=0, bytes_accessed=4 * mate.size * 2, transcendentals=0),
        name="join_rows",
    )(straight, mate, ahead)


def group_blocks(refs, roles, first, second):
    me = lax.axis_index("seq")
    core, upper = me & 1, (me // REACH) & 1
    count = roles.shape[1]
    parts = [(ref, at) for ref in refs for at in range(0, ref.shape[0], count)]
    for i, (ref, at) in enumerate(parts):
        roles[(upper ^ (i // 2)) * 2 + (core ^ (i % 2))] = ref[at : at + count]
    first = [ref[...] for ref in first]
    second = [ref[...] for ref in second]
    width = roles.shape[-1]
    mids = switch_tiles([jnp.concatenate([roles[c], roles[2 + c]], axis=-1) for c in range(2)], *first)
    halves = [slice(0, width), slice(width, 2 * width)]
    pairs = [jnp.concatenate([mids[0][:, part], mids[1][:, part]], axis=-1) for part in halves]
    return [o[:, part] for o in switch_tiles(pairs, *second) for part in halves]


def group_kernel(blocks, *refs):
    first, second, out, roles = refs[blocks : blocks + 6], refs[blocks + 6 : blocks + 12], refs[-2], refs[-1]
    for i, end in enumerate(group_blocks(refs[:blocks], roles, first, second)):
        out[i] = end


def last_kernel(blocks, shards, *refs):
    first, second = refs[blocks : blocks + 6], refs[blocks + 6 : blocks + 12]
    done, out, roles, whole, sems = refs[blocks + 12 : -4], refs[-4], refs[-3], refs[-2], refs[-1]
    ends = group_blocks(refs[:blocks], roles, first, second)
    me = lax.axis_index("seq")
    near = (me & (REACH - 1)) >> 1
    tile = shards * shards
    row, col = iota2((tile, tile), 0), iota2((tile, tile), 1)
    group, half, core = col // (4 * shards), (col // (2 * shards)) % 2, (col // shards) % 2
    source = half * REACH + ((group ^ near) * 2 + core)
    place = one_hot((row // shards == col % shards) & (row % shards == source))
    streams, rows, _ = whole.shape
    copies = []
    for s in range(streams):
        for t in range(rows // tile):
            at = s * (rows // shards) + t * shards
            parts = [d[i, at : at + shards] for d in done for i in range(4)]
            parts += [end[at : at + shards] for end in ends]
            to = (s, slice(t * tile, (t + 1) * tile))
            whole[to] = dot(place, jnp.concatenate(parts, axis=0)).astype(jnp.bfloat16)
            copies.append(pltpu.make_async_copy(whole.at[to], out.at[to], sems.at[s, t]))
            copies[-1].start()
    for copy in copies:
        copy.wait()


def run_group(kernel, blocks, count, params, extra, out_shape, out_spec, scratch, name, weigh=1):
    width = blocks[0].shape[-1]
    args = (*blocks, *params, *extra)
    hidden = params[0].shape[1]
    return pl.pallas_call(
        functools.partial(kernel, len(blocks)),
        out_shape=out_shape,
        in_specs=[pl.BlockSpec(memory_space=pltpu.VMEM)] * len(args),
        out_specs=pl.BlockSpec(memory_space=out_spec),
        scratch_shapes=[pltpu.VMEM((4, count, width), jnp.bfloat16), *scratch],
        compiler_params=pltpu.CompilerParams(vmem_limit_bytes=32 * MIB),
        cost_estimate=pl.CostEstimate(
            flops=weigh * 2 * 2 * count * 4 * 2 * width * hidden,
            bytes_accessed=weigh * sum(a.size * a.dtype.itemsize for a in args),
            transcendentals=weigh * 4 * count * hidden,
        ),
        name=name,
    )(*args)


def exchanged(features, params, shards):
    straight, mate, ahead, *firsts = sort_rows(features, shards)
    count, width = straight.shape
    groups = REACH // 2
    got = {}

    def send(value, mask, before=()):
        if before:
            value, *held = lax.optimization_barrier((value, *(got[key] for key in before)))
            got.update(zip(before, held))
        got[mask] = lax.ppermute(value, "seq", [(d, d ^ mask) for d in range(shards)])

    for mask, value in zip(FIRSTS, firsts):
        send(value, mask)
    send(mate, 1)
    joined = join_rows(straight, got[1], ahead)
    got[0] = joined[0]
    ready = dict(zip([*range(2, REACH, 2), *range(REACH + 2, 2 * REACH, 2)], joined[1:]))
    for mask, before in ORDER:
        send(ready[mask], mask, before)
    block = jax.ShapeDtypeStruct((4, count, width), features.dtype)
    whole = jax.ShapeDtypeStruct(features.shape, features.dtype)
    ends = []
    for g in range(groups):
        far = FIRSTS if g == 0 else (REACH + 2 * g,)
        blocks = [got[2 * g], *(got[mask] for mask in far)]
        if g < groups - 1:
            ends.append(
                run_group(group_kernel, blocks, count, params, (), block, pltpu.VMEM, (), "switch_group", WEIGH[g])
            )

    def kernel(blocks, *refs):
        last_kernel(blocks, shards, *refs)

    streams, rows, _ = features.shape
    sems = pltpu.SemaphoreType.DMA((streams, rows // (shards * shards)))
    scratch = (pltpu.VMEM(whole.shape, whole.dtype), sems)
    return run_group(kernel, blocks, count, params, tuple(ends), whole, pltpu.HBM, scratch, "switch_last")


def gathered(features, first, second):
    streams, rows_here, width = features.shape
    devices = lax.axis_size("seq")
    slots = rows_here // devices
    outgoing = features.reshape(streams, slots, devices, width).transpose(2, 0, 1, 3)
    outgoing = outgoing.reshape(devices, streams * slots, width)
    received = lax.all_to_all(outgoing, "seq", split_axis=0, concat_axis=0, tiled=True)
    clusters = devices // (2 * REACH)
    halves = received.reshape(clusters, 2, REACH, streams * slots, width)
    pairs = jnp.concatenate([halves[:, 0], halves[:, 1]], axis=-1).reshape(-1, 2 * width)
    (mid,) = switch_tiles([pairs], *first)
    mid = mid.reshape(clusters, REACH // 2, 2, streams * slots, 2, width)
    pairs = mid.transpose(0, 4, 1, 3, 2, 5).reshape(-1, 2 * width)
    (result,) = switch_tiles([pairs], *second)
    result = result.reshape(devices // 2, streams, slots, 2, width)
    return result.transpose(1, 2, 0, 3, 4).reshape(streams, rows_here, width)


def per_device(features, *params):
    first, second = params[:6], params[6:]
    shards = lax.axis_size("seq")
    if shards == 2 * REACH and features.shape[1] % (shards * shards) == 0:
        return exchanged(features, params, shards)
    return gathered(features, first, second)


def solution(mesh):
    return jax.shard_map(
        per_device,
        mesh=mesh,
        in_specs=(P("groups", "seq", None),) + (P(),) * 12,
        out_specs=P("groups", "seq", None),
        check_vma=False,
    )
```

```python
import functools

import jax
import jax.numpy as jnp
from jax import lax
from jax.experimental import pallas as pl
from jax.experimental.pallas import tpu as pltpu
from jax.sharding import PartitionSpec as P

REACH = 8
FIRSTS = (REACH, REACH + 1)
ORDER = ((10, ()), (2, ()), (12, (8, 9)), (4, (8, 9)), (14, (10,)), (6, (8, 9)))
WEIGH = (0, 0, 1)
MIB = 1 << 20


def gelu(n):
    root = 0.7978845608028654
    half = 0.5 * n
    return half + half * jnp.tanh(n * (root + (root * 0.044715) * (n * n)))


def dot(a, b):
    return jnp.dot(a, b, preferred_element_type=jnp.float32)


def activated(hidden, gain, shift):
    center = hidden - jnp.mean(hidden, axis=-1, keepdims=True)
    spread = jnp.mean(center * center, axis=-1, keepdims=True)
    normed = center * lax.rsqrt(spread + 1e-05) * gain[None] + shift[None]
    return gelu(normed).astype(jnp.bfloat16)


def switch_tiles(tiles, expand, contract, gain, shift, keep, bias):
    keep = jax.nn.sigmoid(keep[None])
    hidden, results = [dot(tiles[0], expand)], []
    for i, s in enumerate(tiles):
        if i + 1 < len(tiles):
            hidden.append(dot(tiles[i + 1], expand))
        active = activated(hidden[i], gain, shift)
        result = keep * s.astype(jnp.float32) + dot(active, contract) + bias[None]
        results.append(result.astype(jnp.bfloat16))
    return results


def iota2(shape, dim):
    return lax.broadcasted_iota(jnp.int32, shape, dim)


def one_hot(hit):
    return jnp.where(hit, 1.0, 0.0).astype(jnp.bfloat16)


def sort_kernel(shards, x_ref, straight, mate, ahead, first, second):
    me = lax.axis_index("seq")
    tile = shards * shards
    streams, rows, _ = x_ref.shape
    row, col = iota2((tile, tile), 0), iota2((tile, tile), 1)
    pick = one_hot((col // shards == row % shards) & (col % shards == ((row // shards) ^ me)))
    for s in range(streams):
        for t in range(rows // tile):
            y = jnp.dot(pick, x_ref[s, t * tile : (t + 1) * tile], preferred_element_type=jnp.float32)
            y = y.astype(jnp.bfloat16)
            at = s * (rows // shards) + t * shards
            for mask in range(shards):
                part = y[mask * shards : (mask + 1) * shards]
                if mask == 0:
                    straight[at : at + shards] = part
                elif mask == REACH:
                    first[at : at + shards] = part
                elif mask == REACH + 1:
                    second[at : at + shards] = part
                elif mask % 2:
                    mate[mask_slot(mask), at : at + shards] = part
                else:
                    ahead[mask_slot(mask) - 1, at : at + shards] = part


def mask_slot(mask):
    chip = mask // 2
    return chip if chip < REACH // 2 else chip - 1


def sort_rows(features, shards):
    streams, rows, width = features.shape
    count = streams * rows // shards
    block = jax.ShapeDtypeStruct((count, width), features.dtype)
    mate = jax.ShapeDtypeStruct((REACH - 1, count, width), features.dtype)
    ahead = jax.ShapeDtypeStruct((REACH - 2, count, width), features.dtype)
    return pl.pallas_call(
        functools.partial(sort_kernel, shards),
        out_shape=[block, mate, ahead, block, block],
        in_specs=[pl.BlockSpec(memory_space=pltpu.VMEM)],
        out_specs=[pl.BlockSpec(memory_space=pltpu.VMEM)] * 5,
        compiler_params=pltpu.CompilerParams(vmem_limit_bytes=16 * MIB),
        cost_estimate=pl.CostEstimate(flops=3 * 10**10, bytes_accessed=2 * features.size * 2, transcendentals=0),
        name="sort_rows",
    )(features)


def join_kernel(straight, mate, ahead, *outs):
    count = straight.shape[0]
    for i, out in enumerate(outs):
        out[:count] = straight[...] if i == 0 else ahead[i - 1]
        out[count:] = mate[i]


def join_rows(straight, mate, ahead):
    count, width = straight.shape
    pair = jax.ShapeDtypeStruct((2 * count, width), straight.dtype)
    return pl.pallas_call(
        join_kernel,
        out_shape=[pair] * (REACH - 1),
        in_specs=[pl.BlockSpec(memory_space=pltpu.VMEM)] * 3,
        out_specs=[pl.BlockSpec(memory_space=pltpu.VMEM)] * (REACH - 1),
        compiler_params=pltpu.CompilerParams(vmem_limit_bytes=16 * MIB),
        cost_estimate=pl.CostEstimate(flops=0, bytes_accessed=4 * mate.size * 2, transcendentals=0),
        name="join_rows",
    )(straight, mate, ahead)


def group_blocks(refs, roles, first, second):
    me = lax.axis_index("seq")
    core, upper = me & 1, (me // REACH) & 1
    count = roles.shape[1]
    parts = [(ref, at) for ref in refs for at in range(0, ref.shape[0], count)]
    for i, (ref, at) in enumerate(parts):
        roles[(upper ^ (i // 2)) * 2 + (core ^ (i % 2))] = ref[at : at + count]
    first = [ref[...] for ref in first]
    second = [ref[...] for ref in second]
    width = roles.shape[-1]
    mids = switch_tiles([jnp.concatenate([roles[c], roles[2 + c]], axis=-1) for c in range(2)], *first)
    halves = [slice(0, width), slice(width, 2 * width)]
    pairs = [jnp.concatenate([mids[0][:, part], mids[1][:, part]], axis=-1) for part in halves]
    return [o[:, part] for o in switch_tiles(pairs, *second) for part in halves]


def placing(shards, first, groups):
    near = (lax.axis_index("seq") & (REACH - 1)) >> 1
    shape = (shards * shards, 4 * shards * groups)
    row, col = iota2(shape, 0), iota2(shape, 1)
    group, half, core = first + col // (4 * shards), (col // (2 * shards)) % 2, (col // shards) % 2
    source = half * REACH + ((group ^ near) * 2 + core)
    return one_hot((row // shards == col % shards) & (row % shards == source))


def group_kernel(blocks, *refs):
    first, second, out, roles = refs[blocks : blocks + 6], refs[blocks + 6 : blocks + 12], refs[-2], refs[-1]
    for i, end in enumerate(group_blocks(refs[:blocks], roles, first, second)):
        out[i] = end


def placing_kernel(blocks, shards, *refs):
    first, second = refs[blocks : blocks + 6], refs[blocks + 6 : blocks + 12]
    done, out, roles = refs[blocks + 12 : -2], refs[-2], refs[-1]
    ends = group_blocks(refs[:blocks], roles, first, second)
    tile = shards * shards
    place = placing(shards, 0, len(done) + 1)
    streams, rows, _ = out.shape
    for s in range(streams):
        for t in range(rows // tile):
            at = s * (rows // shards) + t * shards
            parts = [d[i, at : at + shards] for d in done for i in range(4)]
            parts += [end[at : at + shards] for end in ends]
            y = dot(place, jnp.concatenate(parts, axis=0))
            out[s, t * tile : (t + 1) * tile] = y.astype(jnp.bfloat16)


def last_kernel(blocks, shards, *refs):
    first, second = refs[blocks : blocks + 6], refs[blocks + 6 : blocks + 12]
    placed, out, roles, whole, sems = refs[blocks + 12], refs[-4], refs[-3], refs[-2], refs[-1]
    ends = group_blocks(refs[:blocks], roles, first, second)
    tile = shards * shards
    place = placing(shards, REACH // 2 - 1, 1)
    streams, rows, _ = whole.shape
    copies = []
    for s in range(streams):
        for t in range(rows // tile):
            at = s * (rows // shards) + t * shards
            to = (s, slice(t * tile, (t + 1) * tile))
            y = dot(place, jnp.concatenate([end[at : at + shards] for end in ends], axis=0))
            whole[to] = placed[to] + y.astype(jnp.bfloat16)
            copies.append(pltpu.make_async_copy(whole.at[to], out.at[to], sems.at[s, t]))
            copies[-1].start()
    for copy in copies:
        copy.wait()


def run_group(kernel, blocks, count, params, extra, out_shape, out_spec, scratch, name, weigh=1):
    width = blocks[0].shape[-1]
    args = (*blocks, *params, *extra)
    hidden = params[0].shape[1]
    return pl.pallas_call(
        functools.partial(kernel, len(blocks)),
        out_shape=out_shape,
        in_specs=[pl.BlockSpec(memory_space=pltpu.VMEM)] * len(args),
        out_specs=pl.BlockSpec(memory_space=out_spec),
        scratch_shapes=[pltpu.VMEM((4, count, width), jnp.bfloat16), *scratch],
        compiler_params=pltpu.CompilerParams(vmem_limit_bytes=32 * MIB),
        cost_estimate=pl.CostEstimate(
            flops=weigh * 2 * 2 * count * 4 * 2 * width * hidden,
            bytes_accessed=weigh * sum(a.size * a.dtype.itemsize for a in args),
            transcendentals=weigh * 4 * count * hidden,
        ),
        name=name,
    )(*args)


def exchanged(features, params, shards):
    straight, mate, ahead, *firsts = sort_rows(features, shards)
    count, width = straight.shape
    groups = REACH // 2
    got = {}

    def send(value, mask, before=()):
        if before:
            value, *held = lax.optimization_barrier((value, *(got[key] for key in before)))
            got.update(zip(before, held))
        got[mask] = lax.ppermute(value, "seq", [(d, d ^ mask) for d in range(shards)])

    for mask, value in zip(FIRSTS, firsts):
        send(value, mask)
    send(mate, 1)
    joined = join_rows(straight, got[1], ahead)
    got[0] = joined[0]
    ready = dict(zip([*range(2, REACH, 2), *range(REACH + 2, 2 * REACH, 2)], joined[1:]))
    for mask, before in ORDER:
        send(ready[mask], mask, before)
    block = jax.ShapeDtypeStruct((4, count, width), features.dtype)
    whole = jax.ShapeDtypeStruct(features.shape, features.dtype)
    ends = []

    def placing_part(blocks, *refs):
        placing_kernel(blocks, shards, *refs)

    for g in range(groups):
        far = FIRSTS if g == 0 else (REACH + 2 * g,)
        blocks = [got[2 * g], *(got[mask] for mask in far)]
        if g < groups - 2:
            ends.append(
                run_group(group_kernel, blocks, count, params, (), block, pltpu.VMEM, (), "switch_group", WEIGH[g])
            )
        elif g < groups - 1:
            placed = run_group(placing_part, blocks, count, params, tuple(ends), whole, pltpu.VMEM, (), "switch_place", WEIGH[g])

    def kernel(blocks, *refs):
        last_kernel(blocks, shards, *refs)

    streams, rows, _ = features.shape
    sems = pltpu.SemaphoreType.DMA((streams, rows // (shards * shards)))
    scratch = (pltpu.VMEM(whole.shape, whole.dtype), sems)
    return run_group(kernel, blocks, count, params, (placed,), whole, pltpu.HBM, scratch, "switch_last")


def gathered(features, first, second):
    streams, rows_here, width = features.shape
    devices = lax.axis_size("seq")
    slots = rows_here // devices
    outgoing = features.reshape(streams, slots, devices, width).transpose(2, 0, 1, 3)
    outgoing = outgoing.reshape(devices, streams * slots, width)
    received = lax.all_to_all(outgoing, "seq", split_axis=0, concat_axis=0, tiled=True)
    clusters = devices // (2 * REACH)
    halves = received.reshape(clusters, 2, REACH, streams * slots, width)
    pairs = jnp.concatenate([halves[:, 0], halves[:, 1]], axis=-1).reshape(-1, 2 * width)
    (mid,) = switch_tiles([pairs], *first)
    mid = mid.reshape(clusters, REACH // 2, 2, streams * slots, 2, width)
    pairs = mid.transpose(0, 4, 1, 3, 2, 5).reshape(-1, 2 * width)
    (result,) = switch_tiles([pairs], *second)
    result = result.reshape(devices // 2, streams, slots, 2, width)
    return result.transpose(1, 2, 0, 3, 4).reshape(streams, rows_here, width)


def per_device(features, *params):
    first, second = params[:6], params[6:]
    shards = lax.axis_size("seq")
    if shards == 2 * REACH and features.shape[1] % (shards * shards) == 0:
        return exchanged(features, params, shards)
    return gathered(features, first, second)


def solution(mesh):
    return jax.shard_map(
        per_device,
        mesh=mesh,
        in_specs=(P("groups", "seq", None),) + (P(),) * 12,
        out_specs=P("groups", "seq", None),
        check_vma=False,
    )
```

```python
import functools

import jax
import jax.numpy as jnp
from jax import lax
from jax.experimental import pallas as pl
from jax.experimental.pallas import tpu as pltpu
from jax.sharding import PartitionSpec as P

REACH = 8
FIRSTS = (REACH, REACH + 1)
ORDER = ((10, ()), (2, ()), (12, (8, 9)), (4, (8, 9)), (14, (10,)), (6, (8, 9)))
WEIGH = (0, 0, 1)
MIB = 1 << 20


def gelu(n):
    root = 0.7978845608028654
    half = 0.5 * n
    return half + half * jnp.tanh(n * (root + (root * 0.044715) * (n * n)))


def dot(a, b):
    return jnp.dot(a, b, preferred_element_type=jnp.float32)


def activated(hidden, gain, shift):
    center = hidden - jnp.mean(hidden, axis=-1, keepdims=True)
    spread = jnp.mean(center * center, axis=-1, keepdims=True)
    normed = center * lax.rsqrt(spread + 1e-05) * gain[None] + shift[None]
    return gelu(normed).astype(jnp.bfloat16)


def switch_tiles(tiles, expand, contract, gain, shift, keep, bias):
    keep = jax.nn.sigmoid(keep[None])
    hidden, results = [dot(tiles[0], expand)], []
    for i, s in enumerate(tiles):
        if i + 1 < len(tiles):
            hidden.append(dot(tiles[i + 1], expand))
        active = activated(hidden[i], gain, shift)
        result = keep * s.astype(jnp.float32) + dot(active, contract) + bias[None]
        results.append(result.astype(jnp.bfloat16))
    return results


def iota2(shape, dim):
    return lax.broadcasted_iota(jnp.int32, shape, dim)


def one_hot(hit):
    return jnp.where(hit, 1.0, 0.0).astype(jnp.bfloat16)


def sort_kernel(shards, x_ref, straight, mate, ahead, first, second):
    me = lax.axis_index("seq")
    tile = shards * shards
    streams, rows, _ = x_ref.shape
    row, col = iota2((tile, tile), 0), iota2((tile, tile), 1)
    pick = one_hot((col // shards == row % shards) & (col % shards == ((row // shards) ^ me)))
    for s in range(streams):
        for t in range(rows // tile):
            y = jnp.dot(pick, x_ref[s, t * tile : (t + 1) * tile], preferred_element_type=jnp.float32)
            y = y.astype(jnp.bfloat16)
            at = s * (rows // shards) + t * shards
            for mask in range(shards):
                part = y[mask * shards : (mask + 1) * shards]
                if mask == 0:
                    straight[at : at + shards] = part
                elif mask == REACH:
                    first[at : at + shards] = part
                elif mask == REACH + 1:
                    second[at : at + shards] = part
                elif mask % 2:
                    mate[mask_slot(mask), at : at + shards] = part
                else:
                    ahead[mask_slot(mask) - 1, at : at + shards] = part


def mask_slot(mask):
    chip = mask // 2
    return chip if chip < REACH // 2 else chip - 1


def sort_rows(features, shards):
    streams, rows, width = features.shape
    count = streams * rows // shards
    block = jax.ShapeDtypeStruct((count, width), features.dtype)
    mate = jax.ShapeDtypeStruct((REACH - 1, count, width), features.dtype)
    ahead = jax.ShapeDtypeStruct((REACH - 2, count, width), features.dtype)
    return pl.pallas_call(
        functools.partial(sort_kernel, shards),
        out_shape=[block, mate, ahead, block, block],
        in_specs=[pl.BlockSpec(memory_space=pltpu.VMEM)],
        out_specs=[pl.BlockSpec(memory_space=pltpu.VMEM)] * 5,
        compiler_params=pltpu.CompilerParams(vmem_limit_bytes=16 * MIB),
        cost_estimate=pl.CostEstimate(flops=3 * 10**10, bytes_accessed=2 * features.size * 2, transcendentals=0),
        name="sort_rows",
    )(features)


def join_kernel(straight, mate, ahead, *outs):
    count = straight.shape[0]
    for i, out in enumerate(outs):
        out[:count] = straight[...] if i == 0 else ahead[i - 1]
        out[count:] = mate[i]


def join_rows(straight, mate, ahead):
    count, width = straight.shape
    pair = jax.ShapeDtypeStruct((2 * count, width), straight.dtype)
    return pl.pallas_call(
        join_kernel,
        out_shape=[pair] * (REACH - 1),
        in_specs=[pl.BlockSpec(memory_space=pltpu.VMEM)] * 3,
        out_specs=[pl.BlockSpec(memory_space=pltpu.VMEM)] * (REACH - 1),
        compiler_params=pltpu.CompilerParams(vmem_limit_bytes=16 * MIB),
        cost_estimate=pl.CostEstimate(flops=0, bytes_accessed=4 * mate.size * 2, transcendentals=0),
        name="join_rows",
    )(straight, mate, ahead)


def group_blocks(refs, roles, first, second):
    me = lax.axis_index("seq")
    core, upper = me & 1, (me // REACH) & 1
    count = roles.shape[1]
    parts = [(ref, at) for ref in refs for at in range(0, ref.shape[0], count)]
    for i, (ref, at) in enumerate(parts):
        roles[(upper ^ (i // 2)) * 2 + (core ^ (i % 2))] = ref[at : at + count]
    first = [ref[...] for ref in first]
    second = [ref[...] for ref in second]
    width = roles.shape[-1]
    mids = switch_tiles([jnp.concatenate([roles[c], roles[2 + c]], axis=-1) for c in range(2)], *first)
    halves = [slice(0, width), slice(width, 2 * width)]
    pairs = [jnp.concatenate([mids[0][:, part], mids[1][:, part]], axis=-1) for part in halves]
    return [o[:, part] for o in switch_tiles(pairs, *second) for part in halves]


def placing(shards, first, groups):
    near = (lax.axis_index("seq") & (REACH - 1)) >> 1
    shape = (shards * shards, 4 * shards * groups)
    row, col = iota2(shape, 0), iota2(shape, 1)
    group, half, core = first + col // (4 * shards), (col // (2 * shards)) % 2, (col // shards) % 2
    source = half * REACH + ((group ^ near) * 2 + core)
    return one_hot((row // shards == col % shards) & (row % shards == source))


def group_kernel(blocks, *refs):
    first, second, out, roles = refs[blocks : blocks + 6], refs[blocks + 6 : blocks + 12], refs[-2], refs[-1]
    for i, end in enumerate(group_blocks(refs[:blocks], roles, first, second)):
        out[i] = end


def placing_kernel(blocks, shards, *refs):
    first, second = refs[blocks : blocks + 6], refs[blocks + 6 : blocks + 12]
    done, out, roles = refs[blocks + 12 : -2], refs[-2], refs[-1]
    ends = group_blocks(refs[:blocks], roles, first, second)
    tile = shards * shards
    place = placing(shards, 0, len(done) + 1)
    streams, rows, _ = out.shape
    for s in range(streams):
        for t in range(rows // tile):
            at = s * (rows // shards) + t * shards
            parts = [d[i, at : at + shards] for d in done for i in range(4)]
            parts += [end[at : at + shards] for end in ends]
            y = dot(place, jnp.concatenate(parts, axis=0))
            out[s, t * tile : (t + 1) * tile] = y.astype(jnp.bfloat16)


def last_kernel(blocks, shards, *refs):
    first, second = refs[blocks : blocks + 6], refs[blocks + 6 : blocks + 12]
    placed, out, roles, whole, sems = refs[blocks + 12], refs[-4], refs[-3], refs[-2], refs[-1]
    ends = group_blocks(refs[:blocks], roles, first, second)
    tile = shards * shards
    place = placing(shards, REACH // 2 - 1, 1)
    streams, rows, _ = whole.shape
    copies = []
    width = whole.shape[2]
    for t in range(rows // tile):
        each = [slice(s * (rows // shards) + t * shards, s * (rows // shards) + (t + 1) * shards) for s in range(streams)]
        sides = [jnp.concatenate([end[at] for end in ends], axis=0) for at in each]
        y = dot(place, jnp.concatenate(sides, axis=-1)).astype(jnp.bfloat16)
        for s in range(streams):
            to = (s, slice(t * tile, (t + 1) * tile))
            whole[to] = placed[to] + y[:, s * width : (s + 1) * width]
            copies.append(pltpu.make_async_copy(whole.at[to], out.at[to], sems.at[s, t]))
            copies[-1].start()
    for copy in copies:
        copy.wait()


def run_group(kernel, blocks, count, params, extra, out_shape, out_spec, scratch, name, weigh=1):
    width = blocks[0].shape[-1]
    args = (*blocks, *params, *extra)
    hidden = params[0].shape[1]
    return pl.pallas_call(
        functools.partial(kernel, len(blocks)),
        out_shape=out_shape,
        in_specs=[pl.BlockSpec(memory_space=pltpu.VMEM)] * len(args),
        out_specs=pl.BlockSpec(memory_space=out_spec),
        scratch_shapes=[pltpu.VMEM((4, count, width), jnp.bfloat16), *scratch],
        compiler_params=pltpu.CompilerParams(vmem_limit_bytes=32 * MIB),
        cost_estimate=pl.CostEstimate(
            flops=weigh * 2 * 2 * count * 4 * 2 * width * hidden,
            bytes_accessed=weigh * sum(a.size * a.dtype.itemsize for a in args),
            transcendentals=weigh * 4 * count * hidden,
        ),
        name=name,
    )(*args)


def exchanged(features, params, shards):
    straight, mate, ahead, *firsts = sort_rows(features, shards)
    count, width = straight.shape
    groups = REACH // 2
    got = {}

    def send(value, mask, before=()):
        if before:
            value, *held = lax.optimization_barrier((value, *(got[key] for key in before)))
            got.update(zip(before, held))
        got[mask] = lax.ppermute(value, "seq", [(d, d ^ mask) for d in range(shards)])

    for mask, value in zip(FIRSTS, firsts):
        send(value, mask)
    send(mate, 1)
    joined = join_rows(straight, got[1], ahead)
    got[0] = joined[0]
    ready = dict(zip([*range(2, REACH, 2), *range(REACH + 2, 2 * REACH, 2)], joined[1:]))
    for mask, before in ORDER:
        send(ready[mask], mask, before)
    block = jax.ShapeDtypeStruct((4, count, width), features.dtype)
    whole = jax.ShapeDtypeStruct(features.shape, features.dtype)
    ends = []

    def placing_part(blocks, *refs):
        placing_kernel(blocks, shards, *refs)

    for g in range(groups):
        far = FIRSTS if g == 0 else (REACH + 2 * g,)
        blocks = [got[2 * g], *(got[mask] for mask in far)]
        if g < groups - 2:
            ends.append(
                run_group(group_kernel, blocks, count, params, (), block, pltpu.VMEM, (), "switch_group", WEIGH[g])
            )
        elif g < groups - 1:
            placed = run_group(placing_part, blocks, count, params, tuple(ends), whole, pltpu.VMEM, (), "switch_place", WEIGH[g])

    def kernel(blocks, *refs):
        last_kernel(blocks, shards, *refs)

    streams, rows, _ = features.shape
    sems = pltpu.SemaphoreType.DMA((streams, rows // (shards * shards)))
    scratch = (pltpu.VMEM(whole.shape, whole.dtype), sems)
    return run_group(kernel, blocks, count, params, (placed,), whole, pltpu.HBM, scratch, "switch_last")


def gathered(features, first, second):
    streams, rows_here, width = features.shape
    devices = lax.axis_size("seq")
    slots = rows_here // devices
    outgoing = features.reshape(streams, slots, devices, width).transpose(2, 0, 1, 3)
    outgoing = outgoing.reshape(devices, streams * slots, width)
    received = lax.all_to_all(outgoing, "seq", split_axis=0, concat_axis=0, tiled=True)
    clusters = devices // (2 * REACH)
    halves = received.reshape(clusters, 2, REACH, streams * slots, width)
    pairs = jnp.concatenate([halves[:, 0], halves[:, 1]], axis=-1).reshape(-1, 2 * width)
    (mid,) = switch_tiles([pairs], *first)
    mid = mid.reshape(clusters, REACH // 2, 2, streams * slots, 2, width)
    pairs = mid.transpose(0, 4, 1, 3, 2, 5).reshape(-1, 2 * width)
    (result,) = switch_tiles([pairs], *second)
    result = result.reshape(devices // 2, streams, slots, 2, width)
    return result.transpose(1, 2, 0, 3, 4).reshape(streams, rows_here, width)


def per_device(features, *params):
    first, second = params[:6], params[6:]
    shards = lax.axis_size("seq")
    if shards == 2 * REACH and features.shape[1] % (shards * shards) == 0:
        return exchanged(features, params, shards)
    return gathered(features, first, second)


def solution(mesh):
    return jax.shard_map(
        per_device,
        mesh=mesh,
        in_specs=(P("groups", "seq", None),) + (P(),) * 12,
        out_specs=P("groups", "seq", None),
        check_vma=False,
    )
```
